32 devices in a mesh: leaf: 2 (over core), row: 4 (over y, x), col: 4 (over z).
Axes of the slice: x: 2, y: 2, z: 4, core: 2. Of those that a mesh axis runs over, the one named last changes fastest.
Arguments:
- sketch_leaf: bfloat16 [16384, 256], P(('leaf', 'row'), 'col'), may hold values from -6 to 6
- sketch_sep: bfloat16 [8192, 256], P(('row', 'col')), may hold values from -6 to 6
- leaf_inverse: bfloat16 [16384, 8192], P(('leaf', 'col'), 'row'), as said below
- coupling: bfloat16 [16384, 2048], P(('leaf', 'col'), 'row'), may hold values from -0.0625 to 0.0625
- sep_inverse: bfloat16 [8192, 8192], P('leaf', ('row', 'col'))
- front_map: int32 [2, 16], replicated, may hold values from 0 to 63, as said below
Outputs:
- sketch_out_leaf: float32 [16384, 256], P(('leaf', 'row'), 'col')
- sketch_out_sep: float32 [8192, 256], P(('row', 'col'))
The draws below stay inside these ranges and needn't reach their ends.
Inputs may be any that keep to these rules, and one draw needn't show every extreme that they name: `front_map`: row block q of every section's coupling lies in separator blocks q * 4 to q * 4 + 3. leaf_inverse and sep_inverse are inverses of lower triangular factor blocks (in natural order), stored in block-cyclic order.
All inputs are finite; a program needn't handle non-finite values.
Results may differ from the reference program's by a relative error of at most 0.024.
Values may be sent and summed in bfloat16 or wider, within the bound.
No kernel may reach another device: no remote copies, remote signals or barrier semaphores. Data moves between devices by JAX's collectives and lax.ppermute only.
A program may use at most 64 MiB of HBM per device.

```python
import jax
import jax.numpy as jnp
from jax import lax

LN = 8192
K = 256
BLK = 128
GROUP = 4
NBB = 16
NB = 2048
NSB = 64
NS = 8192
N_LEAF = 2
N_ROW = 4
N_COL = 4


def natural_order(count, parts, block):
    index = jnp.arange(count, dtype=jnp.int32)
    share = count // parts
    owner = index // share
    inside = index % share
    return (inside // block * parts + owner) * block + inside % block


def triangle_inverse(key, count, row_parts, col_parts):
    row_nat = natural_order(count, row_parts, BLK)
    col_nat = natural_order(count, col_parts, BLK)
    key_off, key_diag = jax.random.split(key)
    values = jax.random.normal(key_off, (count, count), jnp.float32) * (0.8 / count ** 0.5)
    diag_vals = 1.0 + 0.5 * jax.random.uniform(key_diag, (count, count), jnp.float32)
    lower = row_nat[:, None] > col_nat[None, :]
    on_diag = row_nat[:, None] == col_nat[None, :]
    return jnp.where(on_diag, diag_vals, jnp.where(lower, values, 0.0))


def draw_leaf_inverse(key, part):
    keys = jax.random.split(jax.random.fold_in(key, 11), N_LEAF)

    def one_section(sub_key):
        return triangle_inverse(sub_key, LN, N_COL, N_ROW).astype(jnp.bfloat16)
    blocks = lax.map(one_section, keys)
    return blocks.reshape(N_LEAF * LN, LN)


def draw_sep_inverse(key, part):
    return triangle_inverse(jax.random.fold_in(key, 23), NS, N_LEAF, N_ROW * N_COL).astype(jnp.bfloat16)


def draw_front_map(key, part):
    slots = jax.random.randint(jax.random.fold_in(key, 37), (N_LEAF, NBB), 0, GROUP, dtype=jnp.int32)
    return jnp.arange(NBB, dtype=jnp.int32)[None, :] * GROUP + slots


def shard_levels(own_key, shape, shards, low, high):
    gain = 1.0
    for axis_at, blocks in shards:
        heights = jax.random.uniform(jax.random.fold_in(jax.random.fold_in(own_key, 6), axis_at), (blocks,), jnp.float32, low / len(shards), high / len(shards))
        gain = gain * jnp.repeat(jnp.exp(heights), shape[axis_at] // blocks).reshape((-1,) + (1,) * (len(shape) - 1 - axis_at))
    return gain


def gaussian(rng, shape, spread, bound, pieces=(), held_as=jnp.bfloat16):
    values = jax.random.normal(rng, shape, jnp.float32) * spread
    if len(pieces) > 0:
        values = shard_levels(rng, shape, pieces, -0.22, 0.18) * values
    return jnp.clip(values, min=-bound, max=bound).astype(held_as)


def setup_inputs(seed: int = 0) -> dict:
    arg_keys = jax.random.split(jax.random.key(seed), 7)
    sketch_leaf = gaussian(arg_keys[0], (N_LEAF * LN, K), 1.0, 6.0, ((0, 8), (1, 4)))
    sketch_sep = gaussian(arg_keys[1], (NS, K), 1.0, 6.0, ((0, 16),))
    leaf_inverse = draw_leaf_inverse(jax.random.fold_in(arg_keys[6], 71), 0)
    coupling = gaussian(arg_keys[3], (N_LEAF * LN, NB), LN ** -0.5, 0.0625, ((0, 8), (1, 4)))
    sep_inverse = draw_sep_inverse(jax.random.fold_in(arg_keys[6], 71), 0)
    front_map = draw_front_map(jax.random.fold_in(arg_keys[6], 71), 0)
    return dict(sketch_leaf=sketch_leaf, sketch_sep=sketch_sep, leaf_inverse=leaf_inverse, coupling=coupling, sep_inverse=sep_inverse, front_map=front_map)


def contract_rows(left, right):
    return lax.dot_general(left, right, (((0,), (0,)), ((), ())), preferred_element_type=jnp.float32)


def reference(sketch_leaf, sketch_sep, leaf_inverse, coupling, sep_inverse, front_map):
    sketch_blocks = sketch_leaf.reshape(N_LEAF, LN, K)
    inverse_blocks = leaf_inverse.reshape(N_LEAF, LN, LN)
    coupling_blocks = coupling.reshape(N_LEAF, LN, NB)

    def forward(items):
        inverse_s, sketch_s, coupling_s = items
        front_z = jnp.dot(inverse_s, sketch_s, preferred_element_type=jnp.float32).astype(jnp.bfloat16)
        coupled = contract_rows(coupling_s, front_z).astype(jnp.bfloat16)
        return front_z, coupled

    front_z, coupled = lax.map(forward, (inverse_blocks, sketch_blocks, coupling_blocks))
    place = (front_map[:, :, None] == jnp.arange(NSB, dtype=jnp.int32)[None, None, :]).astype(jnp.float32)
    coupled_wide = coupled.astype(jnp.float32).reshape(N_LEAF, NBB, BLK, K)
    total = jnp.einsum("sqb,sqik->bik", place, coupled_wide).reshape(NS, K)
    sep_rhs = (sketch_sep.astype(jnp.float32) - total).astype(jnp.bfloat16)
    sep_mid = jnp.dot(sep_inverse, sep_rhs, preferred_element_type=jnp.float32).astype(jnp.bfloat16)
    sketch_out_sep = contract_rows(sep_inverse, sep_mid)
    sep_round = sketch_out_sep.astype(jnp.bfloat16).reshape(NSB, BLK, K)
    pulled = sep_round[front_map.astype(jnp.int32)].reshape(N_LEAF, NB, K)

    def backward(items):
        inverse_s, coupling_s, front_s, pulled_s = items
        update = jnp.dot(coupling_s, pulled_s, preferred_element_type=jnp.float32)
        leaf_rhs = (front_s.astype(jnp.float32) - update).astype(jnp.bfloat16)
        return contract_rows(inverse_s, leaf_rhs)

    sketch_out_leaf = lax.map(backward, (inverse_blocks, coupling_blocks, front_z, pulled))
    return sketch_out_leaf.reshape(N_LEAF * LN, K), sketch_out_sep
```

```python
import jax
import jax.numpy as jnp
from jax import lax
from jax.experimental import pallas as pl
from jax.experimental.pallas import tpu as pltpu
from jax.sharding import PartitionSpec as P

STREAMS = 1
TILE = 256
F32 = jnp.float32
BF16 = jnp.bfloat16


def dot_nt(left, right):
    return lax.dot_general(left, right, (((1,), (1,)), ((), ())), preferred_element_type=F32)


def dot_nn(left, right):
    return lax.dot_general(left, right, (((1,), (0,)), ((), ())), preferred_element_type=F32)


def call(kernel, outs, index, operands, scratch, flops, name):
    vmem = pl.BlockSpec(memory_space=pltpu.VMEM)
    moved = sum(a.size * a.dtype.itemsize for a in operands)
    return pl.pallas_call(
        kernel,
        out_shape=outs,
        in_specs=[pl.BlockSpec(memory_space=pltpu.SMEM)] + [vmem] * len(operands),
        out_specs=[vmem] * len(outs),
        scratch_shapes=scratch,
        cost_estimate=pl.CostEstimate(flops=flops, bytes_accessed=moved, transcendentals=0),
        name=name,
    )(index, *operands)


def exchange(pieces, axis):
    size = lax.axis_size(axis)
    out = [pieces[0]]
    for o in range(1, size):
        out.append(lax.ppermute(pieces[o], axis, [(i, i ^ o) for i in range(size)]))
    return out


def spread(piece, axis):
    return exchange([piece] * lax.axis_size(axis), axis)


def add_all(pieces):
    total = pieces[0].astype(F32)
    for piece in pieces[1:]:
        total = total + piece.astype(F32)
    return total


def at(index, step):
    return pl.ds(pl.multiple_of(index * step, step), step)


def shards(sketch_leaf, sketch_sep, leaf_inverse, coupling, sep_inverse, front_map):
    n_leaf, n_row, n_col = (lax.axis_size(a) for a in ("leaf", "row", "col"))
    assert n_row == n_col and n_row & (n_row - 1) == 0 and n_leaf & (n_leaf - 1) == 0
    n = n_row
    section, r, c = (lax.axis_index(a) for a in ("leaf", "row", "col"))
    q = r * n_col + c
    rows, width = leaf_inverse.shape
    own_columns = sketch_leaf.shape[1]
    chunk = own_columns // STREAMS
    cols = chunk * n
    blk = coupling.shape[1] * n_row // front_map.shape[1]
    span = coupling.shape[1]
    sep_rows, sep_width = sep_inverse.shape
    group = sketch_sep.shape[0] // blk
    part = sep_rows // n_col

    slots = [
        jnp.clip(front_map[section ^ o, q] - q * group, 0, group - 1) for o in range(n_leaf)
    ]
    index = jnp.stack([r, c] + slots).astype(jnp.int32)

    def needed(row_end, row_parts, col_parts, limit):
        last = (row_end // blk) * row_parts - 1
        return min(limit, (last // col_parts + 1) * blk)

    def first_row(col_start, row_parts, col_parts, limit):
        return min(limit, (col_start // blk) * col_parts // row_parts * blk)

    def forward_leaf(idx, inv, *refs):
        pieces, outs, lhs = refs[:n], refs[n : 2 * n], refs[2 * n]
        for o in range(n):
            lhs[at(idx[0] ^ o, chunk), :] = pieces[o][...]
        for start in range(0, rows, TILE):
            reach = needed(start + TILE, n_col, n_row, width)
            acc = dot_nt(lhs[:, :reach], inv[start : start + TILE, :reach]).astype(BF16)
            for p in range(n):
                outs[p][:, start : start + TILE] = acc[p * chunk : (p + 1) * chunk]

    def forward_coupling(idx, cpl, *refs):
        pieces, outs, lhs, res = refs[:n], refs[n : 2 * n], refs[2 * n], refs[2 * n + 1]
        for p in range(n):
            lhs[at(idx[0] ^ idx[1] ^ p, chunk), :] = pieces[p][...]
        for start in range(0, span, TILE):
            res[:, start : start + TILE] = dot_nn(lhs[...], cpl[:, start : start + TILE])
        for o in range(n):
            outs[o][...] = res[:, at(idx[1] ^ o, blk)].astype(BF16)

    def forward_sep(idx, inv, sketch, *refs):
        blocks, outs = refs[:n_leaf], refs[n_leaf : n_leaf + n]
        rhs, lhs = refs[n_leaf + n :]
        rhs[...] = sketch[...].astype(F32)
        for o in range(n_leaf):
            place = at(idx[2 + o], blk)
            rhs[:, place] = rhs[:, place] - blocks[o][...].astype(F32)
        for k in range(n):
            lhs[at(idx[0] ^ k, chunk), :] = rhs[k * chunk : (k + 1) * chunk, :].astype(BF16)
        for start in range(0, sep_rows, TILE):
            reach = needed(start + TILE, n_leaf, n_row * n_col, sep_width)
            acc = dot_nt(lhs[:, :reach], inv[start : start + TILE, :reach]).astype(BF16)
            for p in range(n):
                outs[p][:, start : start + TILE] = acc[p * chunk : (p + 1) * chunk]

    def reduce_row(idx, *refs):
        pieces, outs = refs[:n], refs[n:]
        for o in range(n):
            place = at(idx[1] ^ o, part)
            outs[o][...] = add_all([piece[:, place] for piece in pieces]).astype(BF16)

    def backward_sep(idx, inv, *refs):
        pieces, out, lhs = refs[: n * n], refs[n * n], refs[n * n + 1]
        for o in range(n):
            for p in range(n):
                lhs[at(idx[0] ^ p, chunk), at(idx[1] ^ o, part)] = pieces[o * n + p][...]
        for start in range(0, sep_width, blk):
            first = first_row(start, n_leaf, n_row * n_col, sep_rows)
            out[:, start : start + blk] = dot_nn(lhs[:, first:], inv[first:, start : start + blk])

    def pull(idx, *refs):
        parts, out, pulled = refs[:n_leaf], refs[n_leaf], refs[n_leaf + 1]
        out[...] = add_all([part_ref[...] for part_ref in parts])
        pulled[...] = out[:, at(idx[2], blk)].astype(BF16)

    def backward_coupling(idx, cpl, *refs):
        pieces, outs, lhs = refs[:n], refs[n : 2 * n], refs[2 * n]
        for o in range(n):
            for k in range(n):
                lhs[at(idx[0] ^ idx[1] ^ k, chunk), at(idx[1] ^ o, blk)] = pieces[o][
                    k * chunk : (k + 1) * chunk, :
                ]
        for start in range(0, rows, TILE):
            acc = dot_nt(lhs[...], cpl[start : start + TILE, :]).astype(BF16)
            for p in range(n):
                outs[p][:, start : start + TILE] = acc[p * chunk : (p + 1) * chunk]

    def backward_leaf(idx, inv, *refs):
        pieces, outs, lhs = refs[:n], refs[n : 2 * n], refs[2 * n]
        for p in range(n):
            lhs[at(idx[0] ^ p, chunk), :] = pieces[p][...]
        for start in range(0, width, TILE):
            first = first_row(start, n_col, n_row, rows)
            acc = dot_nn(lhs[:, first:], inv[first:, start : start + TILE]).astype(BF16)
            for o in range(n):
                outs[o][:, start : start + TILE] = acc[o * chunk : (o + 1) * chunk]

    def shape(*dims, dtype=BF16):
        return jax.ShapeDtypeStruct(dims, dtype)

    leaf_t = sketch_leaf.T
    sep_t = sketch_sep.T.reshape(n, STREAMS, chunk, sep_width)

    def stream(h):
        own = leaf_t[h * chunk : (h + 1) * chunk]
        panels = [shape(chunk, rows)] * n
        parts = call(
            forward_leaf, panels, index, [leaf_inverse] + spread(own, "col"),
            [pltpu.VMEM((cols, width), BF16)], 2 * cols * rows * width, "forward_leaf",
        )
        front = add_all(exchange(parts, "row")).astype(BF16)
        parts = call(
            forward_coupling, [shape(cols, blk)] * n, index, [coupling] + spread(front, "row"),
            [pltpu.VMEM((cols, rows), BF16), pltpu.VMEM((cols, span), F32)],
            2 * cols * rows * span, "forward_coupling",
        )
        coupled = add_all(exchange(parts, "col")).astype(BF16)
        sketch = sep_t[:, h].reshape(cols, sep_width)
        parts = call(
            forward_sep, [shape(chunk, sep_rows)] * n, index,
            [sep_inverse, sketch] + spread(coupled, "leaf"),
            [pltpu.VMEM((cols, sep_width), F32), pltpu.VMEM((cols, sep_width), BF16)],
            2 * cols * sep_rows * sep_width, "forward_sep",
        )
        parts = call(
            reduce_row, [shape(chunk, part)] * n, index, exchange(parts, "row"), [],
            4 * chunk * sep_rows, "reduce_row",
        )
        mid = add_all(exchange(parts, "col")).astype(BF16)
        pieces = []
        for piece in spread(mid, "col"):
            pieces += spread(piece, "row")
        (part_out,) = call(
            backward_sep, [shape(cols, sep_width, dtype=F32)], index, [sep_inverse] + pieces,
            [pltpu.VMEM((cols, sep_rows), BF16)], 2 * cols * sep_rows * sep_width, "backward_sep",
        )
        out_sep, pulled = call(
            pull, [shape(cols, sep_width, dtype=F32), shape(cols, blk)], index,
            spread(part_out, "leaf"), [], cols * sep_width, "pull",
        )
        parts = call(
            backward_coupling, panels, index, [coupling] + spread(pulled, "col"),
            [pltpu.VMEM((cols, span), BF16)], 2 * cols * rows * span, "backward_coupling",
        )
        back = add_all(exchange(parts, "row"))
        leaf_rhs = (front.astype(F32) - back).astype(BF16)
        parts = call(
            backward_leaf, panels, index, [leaf_inverse] + spread(leaf_rhs, "row"),
            [pltpu.VMEM((cols, rows), BF16)], 2 * cols * rows * width, "backward_leaf",
        )
        return add_all(exchange(parts, "col")), out_sep

    results = [stream(h) for h in range(STREAMS)]
    out_leaf = jnp.concatenate([leaf for leaf, _ in results], axis=0)
    out_sep = jnp.stack([sep.reshape(n, chunk, sep_width) for _, sep in results], axis=1)
    return out_leaf.T, out_sep.reshape(n * own_columns, sep_width).T


def solution(mesh):
    placed = (
        P(("leaf", "row"), "col"),
        P(("row", "col"), None),
        P(("leaf", "col"), "row"),
        P(("leaf", "col"), "row"),
        P("leaf", ("row", "col")),
        P(),
    )
    return jax.shard_map(
        shards,
        mesh=mesh,
        in_specs=placed,
        out_specs=(P(("leaf", "row"), "col"), P(("row", "col"), None)),
        check_vma=False,
    )
```

```python
import jax
import jax.numpy as jnp
from jax import lax
from jax.experimental import pallas as pl
from jax.experimental.pallas import tpu as pltpu
from jax.sharding import PartitionSpec as P


PHASES = 1
STREAMS = 2
KERNEL_BYTES = 24 << 20
TILE = 256
COVER = 40
SETTLE = 10**10
F32 = jnp.float32
BF16 = jnp.bfloat16


def dot_nt(left, right):
    return lax.dot_general(left, right, (((1,), (1,)), ((), ())), preferred_element_type=F32)


def dot_nn(left, right):
    return lax.dot_general(left, right, (((1,), (0,)), ((), ())), preferred_element_type=F32)


def call(kernel, outs, index, operands, scratch, flops):
    moved = sum(a.size * a.dtype.itemsize for a in operands)
    return pl.pallas_call(
        kernel,
        out_shape=outs,
        in_specs=[pl.BlockSpec(memory_space=pltpu.SMEM)]
        + [pl.BlockSpec(memory_space=pltpu.VMEM)] * len(operands),
        out_specs=[pl.BlockSpec(memory_space=pltpu.VMEM)] * len(outs),
        scratch_shapes=scratch,
        cost_estimate=pl.CostEstimate(flops=flops, bytes_accessed=moved, transcendentals=0),
        compiler_params=pltpu.CompilerParams(vmem_limit_bytes=KERNEL_BYTES),
    )(index, *operands)


def after(value, *done):
    return lax.optimization_barrier((value, *done))[0]


def settle(index):
    def kernel(index, out):
        for k in range(index.shape[0]):
            out[k] = index[k]

    return pl.pallas_call(
        kernel,
        out_shape=jax.ShapeDtypeStruct(index.shape, index.dtype),
        in_specs=[pl.BlockSpec(memory_space=pltpu.SMEM)],
        out_specs=pl.BlockSpec(memory_space=pltpu.SMEM),
        cost_estimate=pl.CostEstimate(flops=SETTLE, bytes_accessed=64, transcendentals=0),
        name="settle",
    )(index)


def exchange(pieces, axis):
    size = lax.axis_size(axis)
    out = [pieces[0]]
    for o in range(1, size):
        out.append(lax.ppermute(pieces[o], axis, [(i, i ^ o) for i in range(size)]))
    return out


def spread(piece, axis):
    return exchange([piece] * lax.axis_size(axis), axis)


def add_all(pieces):
    total = pieces[0].astype(F32)
    for piece in pieces[1:]:
        total = total + piece.astype(F32)
    return total


def at(index, step):
    return pl.ds(pl.multiple_of(index * step, step), step)


def shape(*dims, dtype=BF16):
    return jax.ShapeDtypeStruct(dims, dtype)


def shards(sketch_leaf, sketch_sep, leaf_inverse, coupling, sep_inverse, front_map):
    n_leaf, n_row, n_col = (lax.axis_size(a) for a in ("leaf", "row", "col"))
    assert n_row == n_col and n_row & (n_row - 1) == 0 and n_leaf & (n_leaf - 1) == 0
    n = n_row
    section, r, c = (lax.axis_index(a) for a in ("leaf", "row", "col"))
    q = r * n_col + c
    rows, width = leaf_inverse.shape
    chunk = sketch_leaf.shape[1] // STREAMS
    cols = chunk * n
    blk = coupling.shape[1] * n_row // front_map.shape[1]
    span = coupling.shape[1]
    sep_rows, sep_width = sep_inverse.shape
    group = sketch_sep.shape[0] // blk
    half = rows // PHASES
    assert rows == width

    slots = [
        jnp.clip(front_map[section ^ o, q] - q * group, 0, group - 1) for o in range(n_leaf)
    ]
    index = settle(jnp.stack([r, c] + slots).astype(jnp.int32))

    def needed(row_end, row_parts, col_parts, limit):
        last = (row_end // blk) * row_parts - 1
        return min(limit, (last // col_parts + 1) * blk)

    def first_row(col_start, row_parts, col_parts, limit):
        return min(limit, (col_start // blk) * col_parts // row_parts * blk)

    def forward_leaf(h, index):
        base = h * half
        depth = needed(base + half, n_col, n_row, width)
        assert depth <= (h + 1) * half

        def kernel(idx, inv, *refs):
            count = n * (h + 1)
            pieces, outs, lhs = refs[:count], refs[count : count + n], refs[count + n]
            for k in range(h + 1):
                for o in range(n):
                    lhs[at(idx[0] ^ o, chunk), k * half : (k + 1) * half] = pieces[k * n + o][...]
            for start in range(0, half, TILE):
                reach = needed(base + start + TILE, n_col, n_row, width)
                acc = dot_nt(
                    lhs[:, :reach], inv[base + start : base + start + TILE, :reach]
                ).astype(BF16)
                for p in range(n):
                    outs[p][:, start : start + TILE] = acc[p * chunk : (p + 1) * chunk]

        return lambda pieces: call(
            kernel, [shape(chunk, half)] * n, index, [leaf_inverse] + pieces,
            [pltpu.VMEM((cols, (h + 1) * half), BF16)], 2 * cols * half * depth,
        )

    def forward_coupling(pieces):
        def kernel(idx, cpl, *refs):
            count = n * PHASES
            pieces, outs = refs[:count], refs[count : count + n]
            lhs, res = refs[count + n :]
            for k in range(PHASES):
                for p in range(n):
                    place = at(idx[0] ^ idx[1] ^ p, chunk)
                    lhs[place, k * half : (k + 1) * half] = pieces[k * n + p][...]
            for s in range(0, span, TILE):
                res[:, s : s + TILE] = dot_nn(lhs[...], cpl[:, s : s + TILE])
            for o in range(n):
                outs[o][...] = res[:, at(idx[1] ^ o, blk)].astype(BF16)

        return call(
            kernel, [shape(cols, blk)] * n, index, [coupling] + pieces,
            [pltpu.VMEM((cols, rows), BF16), pltpu.VMEM((cols, span), F32)],
            COVER * cols * rows * span,
        )

    def sep_rhs(sketch, blocks):
        def kernel(idx, sketch, *refs):
            blocks, outs, rhs = refs[:n_leaf], refs[n_leaf:-1], refs[-1]
            rhs[...] = sketch[...].astype(F32)
            for o in range(n_leaf):
                place = at(idx[2 + o], blk)
                rhs[:, place] = rhs[:, place] - blocks[o][...].astype(F32)
            for k in range(n):
                rounded = rhs[k * chunk : (k + 1) * chunk, :].astype(BF16)
                for axis in range(2):
                    outs[axis][at(idx[axis] ^ k, chunk), :] = rounded

        return call(
            kernel, [shape(cols, sep_width)] * 2, index, [sketch] + blocks,
            [pltpu.VMEM((cols, sep_width), F32)], cols * sep_width,
        )

    def forward_sep(index, base, size, rhs):
        def kernel(idx, inv, lhs, *outs):
            for start in range(0, size, TILE):
                reach = needed(base + start + TILE, n_leaf, n_row * n_col, sep_width)
                acc = dot_nt(
                    lhs[:, :reach], inv[base + start : base + start + TILE, :reach]
                ).astype(BF16)
                for p in range(n):
                    outs[p][:, start : start + TILE] = acc[p * chunk : (p + 1) * chunk]

        return call(
            kernel, [shape(chunk, size)] * n, index, [sep_inverse, rhs], [],
            2 * cols * size * sep_width,
        )

    def reduce_first(size, second, pieces):
        part = size // n

        def kernel(idx, *refs):
            pieces, outs = refs[:n], refs[n:]
            for o in range(n):
                place = at(idx[second] ^ o, part)
                outs[o][...] = add_all([piece[:, place] for piece in pieces]).astype(BF16)

        return call(kernel, [shape(chunk, part)] * n, index, pieces, [], n * chunk * size)

    def backward_sep(base, size, first_axis, pieces, before):
        part = size // n
        given = [] if before is None else [before]

        def kernel(idx, inv, *refs):
            pieces, before, (out, lhs) = refs[:n], refs[n:-2], refs[-2:]
            for p in range(n):
                for o in range(n):
                    place = at(idx[first_axis] ^ p, chunk), at(idx[1 - first_axis] ^ o, part)
                    lhs[place] = pieces[p][o]
            for start in range(0, sep_width, TILE):
                first = max(first_row(start, n_leaf, n_row * n_col, sep_rows) - base, 0)
                stop = start + TILE
                if first < size:
                    acc = dot_nn(lhs[:, first:], inv[base + first : base + size, start:stop])
                else:
                    acc = jnp.zeros((cols, TILE), F32)
                for old in before:
                    acc = acc + old[:, start:stop]
                out[:, start:stop] = acc

        return call(
            kernel, [shape(cols, sep_width, dtype=F32)], index, [sep_inverse] + pieces + given,
            [pltpu.VMEM((cols, size), BF16)], 2 * cols * size * sep_width,
        )[0]

    def pull(parts):
        def kernel(idx, *refs):
            parts, out, pulled = refs[:n_leaf], refs[n_leaf], refs[n_leaf + 1]
            out[...] = add_all([ref[...] for ref in parts])
            pulled[...] = out[:, at(idx[2], blk)].astype(BF16)

        return call(
            kernel, [shape(cols, sep_width, dtype=F32), shape(cols, blk)], index, parts, [],
            cols * sep_width,
        )

    def backward_coupling(h, pieces):
        base = h * half

        def kernel(idx, cpl, *refs):
            pieces, outs, lhs = refs[:n], refs[n : 2 * n], refs[2 * n]
            for o in range(n):
                for k in range(n):
                    lhs[at(idx[0] ^ idx[1] ^ k, chunk), at(idx[1] ^ o, blk)] = pieces[o][
                        k * chunk : (k + 1) * chunk, :
                    ]
            for start in range(0, half, TILE):
                acc = dot_nt(lhs[...], cpl[base + start : base + start + TILE, :]).astype(BF16)
                for p in range(n):
                    outs[p][:, start : start + TILE] = acc[p * chunk : (p + 1) * chunk]

        return call(
            kernel, [shape(chunk, half)] * n, index, [coupling] + pieces,
            [pltpu.VMEM((cols, span), BF16)], COVER * cols * half * span,
        )

    def backward_leaf(index, h, pieces):
        base = h * half
        later = PHASES - h

        def kernel(idx, inv, *refs):
            count = n * later
            pieces, outs, lhs = refs[:count], refs[count : count + n], refs[count + n]
            for k in range(later):
                for p in range(n):
                    lhs[at(idx[0] ^ p, chunk), k * half : (k + 1) * half] = pieces[k * n + p][...]
            for start in range(0, half, TILE):
                first = first_row(base + start, n_col, n_row, rows)
                assert first >= base
                acc = dot_nn(
                    lhs[:, first - base :], inv[first:, base + start : base + start + TILE]
                ).astype(BF16)
                for o in range(n):
                    outs[o][:, start : start + TILE] = acc[o * chunk : (o + 1) * chunk]

        return call(
            kernel, [shape(chunk, half)] * n, index, [leaf_inverse] + pieces,
            [pltpu.VMEM((cols, later * half), BF16)], 2 * cols * half * half * later,
        )

    leaf_t = sketch_leaf.T
    sep_t = sketch_sep.T.reshape(n, STREAMS, chunk, sep_width)

    def stream(h):
        source = leaf_t[h * chunk : (h + 1) * chunk]
        if h:
            source = after(source, *arrived[-1][1:])
        pieces = spread(source, "col")
        arrived.append(pieces)
        parts = forward_leaf(0, index)(pieces)
        front = add_all(exchange(parts, "row")).astype(BF16)
        parts = forward_coupling(spread(front, "row"))
        coupled = add_all(exchange(parts, "col")).astype(BF16)
        sketch = sep_t[:, h].reshape(cols, sep_width)
        rhs = sep_rhs(sketch, spread(coupled, "leaf"))
        parts = exchange(forward_sep(index, 0, sep_rows, rhs[0]), "row")
        parts = exchange(reduce_first(sep_rows, 1, parts), "col")
        mid = add_all(parts).astype(BF16)
        pieces = spread(jnp.stack(spread(mid, "col")), "row")
        total = backward_sep(0, sep_rows, 0, pieces, None)
        out_sep, pulled = pull(spread(total, "leaf"))
        parts = backward_coupling(0, spread(pulled, "col"))
        back = add_all(exchange(parts, "row"))
        leaf_rhs = (front.astype(F32) - back).astype(BF16)
        parts = backward_leaf(index, 0, spread(leaf_rhs, "row"))
        return add_all(exchange(parts, "col")), out_sep

    arrived = []
    results = [stream(h) for h in range(STREAMS)]
    out_leaf = jnp.concatenate([leaf for leaf, _ in results], axis=0)
    out_sep = jnp.stack([sep.reshape(n, chunk, sep_width) for _, sep in results], axis=1)
    return out_leaf.T, out_sep.reshape(sketch_sep.shape[1], sep_width).T


def solution(mesh):
    placed = (
        P(("leaf", "row"), "col"),
        P(("row", "col"), None),
        P(("leaf", "col"), "row"),
        P(("leaf", "col"), "row"),
        P("leaf", ("row", "col")),
        P(),
    )

    return jax.shard_map(
        shards,
        mesh=mesh,
        in_specs=placed,
        out_specs=(P(("leaf", "row"), "col"), P(("row", "col"), None)),
        check_vma=False,
    )
```

```python
import jax
import jax.numpy as jnp
from jax import lax
from jax.experimental import pallas as pl
from jax.experimental.pallas import tpu as pltpu
from jax.sharding import PartitionSpec as P


PHASES = 1
STREAMS = 2
KERNEL_BYTES = 24 << 20
TILE = 256
COVER = 40
SETTLE = 10**10
TOUCH = False, False, False, False
F32 = jnp.float32
BF16 = jnp.bfloat16


def dot_nt(left, right):
    return lax.dot_general(left, right, (((1,), (1,)), ((), ())), preferred_element_type=F32)


def dot_nn(left, right):
    return lax.dot_general(left, right, (((1,), (0,)), ((), ())), preferred_element_type=F32)


def call(kernel, outs, index, operands, scratch, flops):
    moved = sum(a.size * a.dtype.itemsize for a in operands)
    return pl.pallas_call(
        kernel,
        out_shape=outs,
        in_specs=[pl.BlockSpec(memory_space=pltpu.SMEM)]
        + [pl.BlockSpec(memory_space=pltpu.VMEM)] * len(operands),
        out_specs=[pl.BlockSpec(memory_space=pltpu.VMEM)] * len(outs),
        scratch_shapes=scratch,
        cost_estimate=pl.CostEstimate(flops=flops, bytes_accessed=moved, transcendentals=0),
        compiler_params=pltpu.CompilerParams(vmem_limit_bytes=KERNEL_BYTES),
    )(index, *operands)


def after(value, *done):
    return lax.optimization_barrier((value, *done))[0]


def settle(index):
    def kernel(index, out):
        for k in range(index.shape[0]):
            out[k] = index[k]

    return pl.pallas_call(
        kernel,
        out_shape=jax.ShapeDtypeStruct(index.shape, index.dtype),
        in_specs=[pl.BlockSpec(memory_space=pltpu.SMEM)],
        out_specs=pl.BlockSpec(memory_space=pltpu.SMEM),
        cost_estimate=pl.CostEstimate(flops=SETTLE, bytes_accessed=64, transcendentals=0),
        name="settle",
    )(index)


def touch(index, panel, done):
    def kernel(index, panel, done, out):
        for k in range(index.shape[0]):
            out[k] = index[k]

    spaces = pltpu.SMEM, pltpu.VMEM, pl.ANY
    return pl.pallas_call(
        kernel,
        out_shape=jax.ShapeDtypeStruct(index.shape, index.dtype),
        in_specs=[pl.BlockSpec(memory_space=space) for space in spaces],
        out_specs=pl.BlockSpec(memory_space=pltpu.SMEM),
        compiler_params=pltpu.CompilerParams(vmem_limit_bytes=KERNEL_BYTES),
        name="touch",
    )(index, panel, done)


def exchange(pieces, axis):
    size = lax.axis_size(axis)
    out = [pieces[0]]
    for o in range(1, size):
        out.append(lax.ppermute(pieces[o], axis, [(i, i ^ o) for i in range(size)]))
    return out


def relay(near, far, axis):
    size = lax.axis_size(axis)
    if size != 4:
        return exchange([near] + [far] * (size - 1), axis)
    out = [near, None, None, None]
    for o, piece in ((3, far), (1, near), (2, None)):
        piece = out[3] if o == 2 else piece
        out[o] = lax.ppermute(piece, axis, [(i, i ^ {1: 1, 2: 1, 3: 3}[o]) for i in range(size)])
    return out


def spread(piece, axis):
    return exchange([piece] * lax.axis_size(axis), axis)


def add_all(pieces):
    total = pieces[0].astype(F32)
    for piece in pieces[1:]:
        total = total + piece.astype(F32)
    return total


def at(index, step):
    return pl.ds(pl.multiple_of(index * step, step), step)


def shape(*dims, dtype=BF16):
    return jax.ShapeDtypeStruct(dims, dtype)


def shards(sketch_leaf, sketch_sep, leaf_inverse, coupling, sep_inverse, front_map):
    n_leaf, n_row, n_col = (lax.axis_size(a) for a in ("leaf", "row", "col"))
    assert n_row == n_col and n_row & (n_row - 1) == 0 and n_leaf & (n_leaf - 1) == 0
    n = n_row
    section, r, c = (lax.axis_index(a) for a in ("leaf", "row", "col"))
    q = r * n_col + c
    rows, width = leaf_inverse.shape
    chunk = sketch_leaf.shape[1] // STREAMS
    cols = chunk * n
    blk = coupling.shape[1] * n_row // front_map.shape[1]
    span = coupling.shape[1]
    sep_rows, sep_width = sep_inverse.shape
    group = sketch_sep.shape[0] // blk
    half = rows // PHASES
    assert rows == width

    slots = [
        jnp.clip(front_map[section ^ o, q] - q * group, 0, group - 1) for o in range(n_leaf)
    ]
    index = settle(jnp.stack([r, c] + slots).astype(jnp.int32))

    def needed(row_end, row_parts, col_parts, limit):
        last = (row_end // blk) * row_parts - 1
        return min(limit, (last // col_parts + 1) * blk)

    def first_row(col_start, row_parts, col_parts, limit):
        return min(limit, (col_start // blk) * col_parts // row_parts * blk)

    def forward_leaf(h, index):
        base = h * half
        depth = needed(base + half, n_col, n_row, width)
        assert depth <= (h + 1) * half

        def kernel(idx, inv, *refs):
            count = n * (h + 1)
            pieces, outs, lhs = refs[:count], refs[count : count + n], refs[count + n]
            for k in range(h + 1):
                for o in range(n):
                    lhs[at(idx[0] ^ o, chunk), k * half : (k + 1) * half] = pieces[k * n + o][...]
            for start in range(0, half, TILE):
                reach = needed(base + start + TILE, n_col, n_row, width)
                acc = dot_nt(
                    lhs[:, :reach], inv[base + start : base + start + TILE, :reach]
                ).astype(BF16)
                for p in range(n):
                    outs[p][:, start : start + TILE] = acc[p * chunk : (p + 1) * chunk]

        return lambda pieces: call(
            kernel, [shape(chunk, half)] * n, index, [leaf_inverse] + pieces,
            [pltpu.VMEM((cols, (h + 1) * half), BF16)], 2 * cols * half * depth,
        )

    def forward_coupling(pieces):
        def kernel(idx, cpl, *refs):
            count = n * PHASES
            pieces, outs = refs[:count], refs[count : count + n]
            lhs, res = refs[count + n :]
            for k in range(PHASES):
                for p in range(n):
                    place = at(idx[0] ^ idx[1] ^ p, chunk)
                    lhs[place, k * half : (k + 1) * half] = pieces[k * n + p][...]
            for s in range(0, span, TILE):
                res[:, s : s + TILE] = dot_nn(lhs[...], cpl[:, s : s + TILE])
            for o in range(n):
                outs[o][...] = res[:, at(idx[1] ^ o, blk)].astype(BF16)

        return call(
            kernel, [shape(cols, blk)] * n, index, [coupling] + pieces,
            [pltpu.VMEM((cols, rows), BF16), pltpu.VMEM((cols, span), F32)],
            COVER * cols * rows * span,
        )

    def sep_rhs(sketch, blocks):
        def kernel(idx, sketch, *refs):
            blocks, outs, rhs = refs[:n_leaf], refs[n_leaf:-1], refs[-1]
            rhs[...] = sketch[...].astype(F32)
            for o in range(n_leaf):
                place = at(idx[2 + o], blk)
                rhs[:, place] = rhs[:, place] - blocks[o][...].astype(F32)
            for k in range(n):
                rounded = rhs[k * chunk : (k + 1) * chunk, :].astype(BF16)
                for axis in range(2):
                    outs[axis][at(idx[axis] ^ k, chunk), :] = rounded

        return call(
            kernel, [shape(cols, sep_width)] * 2, index, [sketch] + blocks,
            [pltpu.VMEM((cols, sep_width), F32)], cols * sep_width,
        )

    def forward_sep(index, base, size, rhs):
        def kernel(idx, inv, lhs, *outs):
            for start in range(0, size, TILE):
                reach = needed(base + start + TILE, n_leaf, n_row * n_col, sep_width)
                acc = dot_nt(
                    lhs[:, :reach], inv[base + start : base + start + TILE, :reach]
                ).astype(BF16)
                for p in range(n):
                    outs[p][:, start : start + TILE] = acc[p * chunk : (p + 1) * chunk]

        return call(
            kernel, [shape(chunk, size)] * n, index, [sep_inverse, rhs], [],
            2 * cols * size * sep_width,
        )

    def reduce_first(size, second, pieces):
        part = size // n

        def kernel(idx, *refs):
            pieces, outs = refs[:n], refs[n:]
            for o in range(n):
                place = at(idx[second] ^ o, part)
                outs[o][...] = add_all([piece[:, place] for piece in pieces]).astype(BF16)

        return call(kernel, [shape(chunk, part)] * n, index, pieces, [], n * chunk * size)

    def backward_sep(base, size, first_axis, pieces, before):
        part = size // n
        given = [] if before is None else [before]

        def kernel(idx, inv, *refs):
            pieces, before, (out, lhs) = refs[:n], refs[n:-2], refs[-2:]
            for p in range(n):
                for o in range(n):
                    place = at(idx[first_axis] ^ p, chunk), at(idx[1 - first_axis] ^ o, part)
                    lhs[place] = pieces[p][o]
            for start in range(0, sep_width, TILE):
                first = max(first_row(start, n_leaf, n_row * n_col, sep_rows) - base, 0)
                stop = start + TILE
                if first < size:
                    acc = dot_nn(lhs[:, first:], inv[base + first : base + size, start:stop])
                else:
                    acc = jnp.zeros((cols, TILE), F32)
                for old in before:
                    acc = acc + old[:, start:stop]
                out[:, start:stop] = acc

        return call(
            kernel, [shape(cols, sep_width, dtype=F32)], index, [sep_inverse] + pieces + given,
            [pltpu.VMEM((cols, size), BF16)], 2 * cols * size * sep_width,
        )[0]

    def pull(parts):
        def kernel(idx, *refs):
            parts, out, pulled = refs[:n_leaf], refs[n_leaf], refs[n_leaf + 1]
            out[...] = add_all([ref[...] for ref in parts])
            pulled[...] = out[:, at(idx[2], blk)].astype(BF16)

        return call(
            kernel, [shape(cols, sep_width, dtype=F32), shape(cols, blk)], index, parts, [],
            cols * sep_width,
        )

    def backward_coupling(h, pieces):
        base = h * half

        def kernel(idx, cpl, *refs):
            pieces, outs, lhs = refs[:n], refs[n : 2 * n], refs[2 * n]
            for o in range(n):
                for k in range(n):
                    lhs[at(idx[0] ^ idx[1] ^ k, chunk), at(idx[1] ^ o, blk)] = pieces[o][
                        k * chunk : (k + 1) * chunk, :
                    ]
            for start in range(0, half, TILE):
                acc = dot_nt(lhs[...], cpl[base + start : base + start + TILE, :]).astype(BF16)
                for p in range(n):
                    outs[p][:, start : start + TILE] = acc[p * chunk : (p + 1) * chunk]

        return call(
            kernel, [shape(chunk, half)] * n, index, [coupling] + pieces,
            [pltpu.VMEM((cols, span), BF16)], COVER * cols * half * span,
        )

    def backward_leaf(index, h, pieces):
        base = h * half
        later = PHASES - h

        def kernel(idx, inv, *refs):
            count = n * later
            pieces, outs, lhs = refs[:count], refs[count : count + n], refs[count + n]
            for k in range(later):
                for p in range(n):
                    lhs[at(idx[0] ^ p, chunk), k * half : (k + 1) * half] = pieces[k * n + p][...]
            for start in range(0, half, TILE):
                first = first_row(base + start, n_col, n_row, rows)
                assert first >= base
                acc = dot_nn(
                    lhs[:, first - base :], inv[first:, base + start : base + start + TILE]
                ).astype(BF16)
                for o in range(n):
                    outs[o][:, start : start + TILE] = acc[o * chunk : (o + 1) * chunk]

        return call(
            kernel, [shape(chunk, half)] * n, index, [leaf_inverse] + pieces,
            [pltpu.VMEM((cols, later * half), BF16)], 2 * cols * half * half * later,
        )

    leaf_t = sketch_leaf.T
    sep_t = sketch_sep.T.reshape(n, STREAMS, chunk, sep_width)

    def stream(h):
        source = leaf_t[h * chunk : (h + 1) * chunk]
        if h:
            source = after(source, seen["A"][1], seen["A"][3])
        pieces = relay(source, source, "col")
        if TOUCH[h]:
            own = touch(index, leaf_inverse, seen["L"] if h else pieces[1])
        else:
            own = index
        seen["A"] = pieces
        parts = forward_leaf(0, own)(pieces)
        seen["L"] = parts[0]
        front = add_all(exchange(parts, "row")).astype(BF16)
        parts = forward_coupling(spread(front, "row"))
        coupled = add_all(exchange(parts, "col")).astype(BF16)
        sketch = sep_t[:, h].reshape(cols, sep_width)
        rhs = sep_rhs(sketch, spread(coupled, "leaf"))
        parts = exchange(forward_sep(index, 0, sep_rows, rhs[0]), "row")
        if h:
            parts = [after(parts[0], seen["mid"])] + parts[1:]
        parts = exchange(reduce_first(sep_rows, 1, parts), "col")
        if h:
            parts = [after(parts[0], seen["stack"])] + parts[1:]
        mid = add_all(parts).astype(BF16)
        stack = jnp.stack(spread(mid, "col"))
        seen["mid"], seen["stack"] = mid, stack
        pieces = spread(stack, "row")
        total = backward_sep(0, sep_rows, 0, pieces, None)
        out_sep, pulled = pull(spread(total, "leaf"))
        parts = backward_coupling(0, spread(pulled, "col"))
        back = add_all(exchange(parts, "row"))
        leaf_rhs = (front.astype(F32) - back).astype(BF16)
        pieces = spread(leaf_rhs, "row")
        own = touch(index, leaf_inverse, leaf_rhs) if TOUCH[2 + h] else index
        parts = backward_leaf(own, 0, pieces)
        return add_all(exchange(parts, "col")), out_sep

    seen = {}
    results = [stream(h) for h in range(STREAMS)]
    out_leaf = jnp.concatenate([leaf for leaf, _ in results], axis=0)
    out_sep = jnp.stack([sep.reshape(n, chunk, sep_width) for _, sep in results], axis=1)
    return out_leaf.T, out_sep.reshape(sketch_sep.shape[1], sep_width).T


def solution(mesh):
    placed = (
        P(("leaf", "row"), "col"),
        P(("row", "col"), None),
        P(("leaf", "col"), "row"),
        P(("leaf", "col"), "row"),
        P("leaf", ("row", "col")),
        P(),
    )

    return jax.shard_map(
        shards,
        mesh=mesh,
        in_specs=placed,
        out_specs=(P(("leaf", "row"), "col"), P(("row", "col"), None)),
        check_vma=False,
    )
```

```python
import jax
import jax.numpy as jnp
from jax import lax
from jax.experimental import pallas as pl
from jax.experimental.pallas import tpu as pltpu
from jax.sharding import PartitionSpec as P


PHASES = 1
SHARES = 1, 1
KERNEL_BYTES = 24 << 20
TILE = 256
COVER = 2
SETTLE = 10**10
TOUCH = False, False, False, False
F32 = jnp.float32
BF16 = jnp.bfloat16


def dot_nt(left, right):
    return lax.dot_general(left, right, (((1,), (1,)), ((), ())), preferred_element_type=F32)


def dot_nn(left, right):
    return lax.dot_general(left, right, (((1,), (0,)), ((), ())), preferred_element_type=F32)


def call(kernel, outs, index, operands, scratch, flops):
    moved = sum(a.size * a.dtype.itemsize for a in operands)
    return pl.pallas_call(
        kernel,
        out_shape=outs,
        in_specs=[pl.BlockSpec(memory_space=pltpu.SMEM)]
        + [pl.BlockSpec(memory_space=pltpu.VMEM)] * len(operands),
        out_specs=[pl.BlockSpec(memory_space=pltpu.VMEM)] * len(outs),
        scratch_shapes=scratch,
        cost_estimate=pl.CostEstimate(flops=flops, bytes_accessed=moved, transcendentals=0),
        compiler_params=pltpu.CompilerParams(vmem_limit_bytes=KERNEL_BYTES),
    )(index, *operands)


def after(value, *done):
    return lax.optimization_barrier((value, *done))[0]


def settle(index):
    def kernel(index, out):
        for k in range(index.shape[0]):
            out[k] = index[k]

    return pl.pallas_call(
        kernel,
        out_shape=jax.ShapeDtypeStruct(index.shape, index.dtype),
        in_specs=[pl.BlockSpec(memory_space=pltpu.SMEM)],
        out_specs=pl.BlockSpec(memory_space=pltpu.SMEM),
        cost_estimate=pl.CostEstimate(flops=SETTLE, bytes_accessed=64, transcendentals=0),
        name="settle",
    )(index)


def touch(index, panel, done):
    def kernel(index, panel, done, out):
        for k in range(index.shape[0]):
            out[k] = index[k]

    spaces = pltpu.SMEM, pltpu.VMEM, pl.ANY
    return pl.pallas_call(
        kernel,
        out_shape=jax.ShapeDtypeStruct(index.shape, index.dtype),
        in_specs=[pl.BlockSpec(memory_space=space) for space in spaces],
        out_specs=pl.BlockSpec(memory_space=pltpu.SMEM),
        compiler_params=pltpu.CompilerParams(vmem_limit_bytes=KERNEL_BYTES),
        name="touch",
    )(index, panel, done)


def exchange(pieces, axis):
    size = lax.axis_size(axis)
    out = [pieces[0]]
    for o in range(1, size):
        out.append(lax.ppermute(pieces[o], axis, [(i, i ^ o) for i in range(size)]))
    return out


def relay(near, far, axis):
    size = lax.axis_size(axis)
    if size != 4:
        return exchange([near] + [far] * (size - 1), axis)
    out = [near, None, None, None]
    for o, piece in ((3, far), (1, near), (2, None)):
        piece = out[3] if o == 2 else piece
        out[o] = lax.ppermute(piece, axis, [(i, i ^ {1: 1, 2: 1, 3: 3}[o]) for i in range(size)])
    return out


def spread(piece, axis):
    return exchange([piece] * lax.axis_size(axis), axis)


def add_all(pieces):
    total = pieces[0].astype(F32)
    for piece in pieces[1:]:
        total = total + piece.astype(F32)
    return total


def at(index, step):
    return pl.ds(pl.multiple_of(index * step, step), step)


def shape(*dims, dtype=BF16):
    return jax.ShapeDtypeStruct(dims, dtype)


def shards(sketch_leaf, sketch_sep, leaf_inverse, coupling, sep_inverse, front_map):
    n_leaf, n_row, n_col = (lax.axis_size(a) for a in ("leaf", "row", "col"))
    assert n_row == n_col and n_row & (n_row - 1) == 0 and n_leaf & (n_leaf - 1) == 0
    n = n_row
    section, r, c = (lax.axis_index(a) for a in ("leaf", "row", "col"))
    q = r * n_col + c
    rows, width = leaf_inverse.shape
    wide = sketch_leaf.shape[1]
    blk = coupling.shape[1] * n_row // front_map.shape[1]
    span = coupling.shape[1]
    sep_rows, sep_width = sep_inverse.shape
    group = sketch_sep.shape[0] // blk
    half = rows // PHASES
    assert rows == width

    slots = [
        jnp.clip(front_map[section ^ o, q] - q * group, 0, group - 1) for o in range(n_leaf)
    ]
    index = settle(jnp.stack([r, c] + slots).astype(jnp.int32))

    leaf_t = sketch_leaf.T
    sep_t = sketch_sep.T.reshape(n, wide, sep_width)

    def stream(h, chunk, offset):
        cols = chunk * n

        def needed(row_end, row_parts, col_parts, limit):
            last = (row_end // blk) * row_parts - 1
            return min(limit, (last // col_parts + 1) * blk)

        def first_row(col_start, row_parts, col_parts, limit):
            return min(limit, (col_start // blk) * col_parts // row_parts * blk)

        def forward_leaf(h, index):
            base = h * half
            depth = needed(base + half, n_col, n_row, width)
            assert depth <= (h + 1) * half

            def kernel(idx, inv, *refs):
                count = n * (h + 1)
                pieces, outs, lhs = refs[:count], refs[count : count + n], refs[count + n]
                for k in range(h + 1):
                    for o in range(n):
                        lhs[at(idx[0] ^ o, chunk), k * half : (k + 1) * half] = pieces[k * n + o][...]
                for start in range(0, half, TILE):
                    reach = needed(base + start + TILE, n_col, n_row, width)
                    acc = dot_nt(
                        lhs[:, :reach], inv[base + start : base + start + TILE, :reach]
                    ).astype(BF16)
                    for p in range(n):
                        outs[p][:, start : start + TILE] = acc[p * chunk : (p + 1) * chunk]

            return lambda pieces: call(
                kernel, [shape(chunk, half)] * n, index, [leaf_inverse] + pieces,
                [pltpu.VMEM((cols, (h + 1) * half), BF16)], 2 * cols * half * depth,
            )

        def forward_coupling(pieces):
            def kernel(idx, cpl, *refs):
                count = n * PHASES
                pieces, outs = refs[:count], refs[count : count + n]
                lhs, res = refs[count + n :]
                for k in range(PHASES):
                    for p in range(n):
                        place = at(idx[0] ^ idx[1] ^ p, chunk)
                        lhs[place, k * half : (k + 1) * half] = pieces[k * n + p][...]
                for s in range(0, span, TILE):
                    res[:, s : s + TILE] = dot_nn(lhs[...], cpl[:, s : s + TILE])
                for o in range(n):
                    outs[o][...] = res[:, at(idx[1] ^ o, blk)].astype(BF16)

            return call(
                kernel, [shape(cols, blk)] * n, index, [coupling] + pieces,
                [pltpu.VMEM((cols, rows), BF16), pltpu.VMEM((cols, span), F32)],
                COVER * cols * rows * span,
            )

        def sep_rhs(sketch, blocks):
            def kernel(idx, sketch, *refs):
                blocks, outs, rhs = refs[:n_leaf], refs[n_leaf:-1], refs[-1]
                rhs[...] = sketch[...].astype(F32)
                for o in range(n_leaf):
                    place = at(idx[2 + o], blk)
                    rhs[:, place] = rhs[:, place] - blocks[o][...].astype(F32)
                for k in range(n):
                    rounded = rhs[k * chunk : (k + 1) * chunk, :].astype(BF16)
                    outs[0][at(idx[0] ^ k, chunk), :] = rounded

            return call(
                kernel, [shape(cols, sep_width)], index, [sketch] + blocks,
                [pltpu.VMEM((cols, sep_width), F32)], cols * sep_width,
            )

        def forward_sep(index, base, size, rhs):
            def kernel(idx, inv, lhs, *outs):
                for start in range(0, size, TILE):
                    reach = needed(base + start + TILE, n_leaf, n_row * n_col, sep_width)
                    acc = dot_nt(
                        lhs[:, :reach], inv[base + start : base + start + TILE, :reach]
                    ).astype(BF16)
                    for p in range(n):
                        outs[p][:, start : start + TILE] = acc[p * chunk : (p + 1) * chunk]

            return call(
                kernel, [shape(chunk, size)] * n, index, [sep_inverse, rhs], [],
                2 * cols * size * sep_width,
            )

        def reduce_first(size, second, pieces):
            part = size // n

            def kernel(idx, *refs):
                pieces, outs = refs[:n], refs[n:]
                for o in range(n):
                    place = at(idx[second] ^ o, part)
                    outs[o][...] = add_all([piece[:, place] for piece in pieces]).astype(BF16)

            return call(kernel, [shape(chunk, part)] * n, index, pieces, [], n * chunk * size)

        def backward_sep(base, size, first_axis, pieces, before):
            part = size // n
            given = [] if before is None else [before]

            def kernel(idx, inv, *refs):
                pieces, before, (out, lhs) = refs[:n], refs[n:-2], refs[-2:]
                for p in range(n):
                    for o in range(n):
                        place = at(idx[first_axis] ^ p, chunk), at(idx[1 - first_axis] ^ o, part)
                        lhs[place] = pieces[p][o]
                for start in range(0, sep_width, TILE):
                    first = max(first_row(start, n_leaf, n_row * n_col, sep_rows) - base, 0)
                    stop = start + TILE
                    if first < size:
                        acc = dot_nn(lhs[:, first:], inv[base + first : base + size, start:stop])
                    else:
                        acc = jnp.zeros((cols, TILE), F32)
                    for old in before:
                        acc = acc + old[:, start:stop]
                    out[:, start:stop] = acc

            return call(
                kernel, [shape(cols, sep_width, dtype=F32)], index, [sep_inverse] + pieces + given,
                [pltpu.VMEM((cols, size), BF16)], 2 * cols * size * sep_width,
            )[0]

        def pull(parts):
            def kernel(idx, *refs):
                parts, out, pulled = refs[:n_leaf], refs[n_leaf], refs[n_leaf + 1]
                out[...] = add_all([ref[...] for ref in parts])
                pulled[...] = out[:, at(idx[2], blk)].astype(BF16)

            return call(
                kernel, [shape(cols, sep_width, dtype=F32), shape(cols, blk)], index, parts, [],
                cols * sep_width,
            )

        def backward_coupling(h, pieces):
            base = h * half

            def kernel(idx, cpl, *refs):
                pieces, outs, lhs = refs[:n], refs[n : 2 * n], refs[2 * n]
                for o in range(n):
                    for k in range(n):
                        lhs[at(idx[0] ^ idx[1] ^ k, chunk), at(idx[1] ^ o, blk)] = pieces[o][
                            k * chunk : (k + 1) * chunk, :
                        ]
                for start in range(0, half, TILE):
                    acc = dot_nt(lhs[...], cpl[base + start : base + start + TILE, :]).astype(BF16)
                    for p in range(n):
                        outs[p][:, start : start + TILE] = acc[p * chunk : (p + 1) * chunk]

            return call(
                kernel, [shape(chunk, half)] * n, index, [coupling] + pieces,
                [pltpu.VMEM((cols, span), BF16)], COVER * cols * half * span,
            )

        def backward_leaf(index, h, pieces):
            base = h * half
            later = PHASES - h

            def kernel(idx, inv, *refs):
                count = n * later
                pieces, outs, lhs = refs[:count], refs[count : count + n], refs[count + n]
                for k in range(later):
                    for p in range(n):
                        lhs[at(idx[0] ^ p, chunk), k * half : (k + 1) * half] = pieces[k * n + p][...]
                for start in range(0, half, TILE):
                    first = first_row(base + start, n_col, n_row, rows)
                    assert first >= base
                    acc = dot_nn(
                        lhs[:, first - base :], inv[first:, base + start : base + start + TILE]
                    ).astype(BF16)
                    for o in range(n):
                        outs[o][:, start : start + TILE] = acc[o * chunk : (o + 1) * chunk]

            return call(
                kernel, [shape(chunk, half)] * n, index, [leaf_inverse] + pieces,
                [pltpu.VMEM((cols, later * half), BF16)], 2 * cols * half * half * later,
            )

        source = leaf_t[offset : offset + chunk]
        if h:
            source = after(source, seen["A"][3])
        pieces = relay(source, source, "col")
        if TOUCH[h]:
            own = touch(index, leaf_inverse, seen["L"] if h else pieces[1])
        else:
            own = index
        seen["A"] = pieces
        parts = forward_leaf(0, own)(pieces)
        seen["L"] = parts[0]
        front = add_all(exchange(parts, "row")).astype(BF16)
        parts = forward_coupling(spread(front, "row"))
        coupled = add_all(exchange(parts, "col")).astype(BF16)
        sketch = sep_t[:, offset : offset + chunk].reshape(cols, sep_width)
        rhs = sep_rhs(sketch, spread(coupled, "leaf"))
        parts = exchange(forward_sep(index, 0, sep_rows, rhs[0]), "row")
        if h:
            parts = [after(parts[0], seen["mid"])] + parts[1:]
        parts = exchange(reduce_first(sep_rows, 1, parts), "col")
        if h:
            parts = [after(parts[0], seen["stack"])] + parts[1:]
        mid = add_all(parts).astype(BF16)
        stack = jnp.stack(spread(mid, "col"))
        seen["mid"], seen["stack"] = mid, stack
        pieces = spread(stack, "row")
        total = backward_sep(0, sep_rows, 0, pieces, None)
        out_sep, pulled = pull(spread(total, "leaf"))
        parts = backward_coupling(0, spread(pulled, "col"))
        back = add_all(exchange(parts, "row"))
        leaf_rhs = (front.astype(F32) - back).astype(BF16)
        pieces = spread(leaf_rhs, "row")
        own = touch(index, leaf_inverse, leaf_rhs) if TOUCH[2 + h] else index
        parts = backward_leaf(own, 0, pieces)
        return add_all(exchange(parts, "col")), out_sep

    seen = {}
    sizes = [wide * share // sum(SHARES) for share in SHARES]
    results = [stream(h, size, sum(sizes[:h])) for h, size in enumerate(sizes)]
    out_leaf = jnp.concatenate([leaf for leaf, _ in results], axis=0)
    out_sep = jnp.concatenate(
        [sep.reshape(n, size, sep_width) for size, (_, sep) in zip(sizes, results)], axis=1
    )
    return out_leaf.T, out_sep.reshape(sketch_sep.shape[1], sep_width).T


def solution(mesh):
    placed = (
        P(("leaf", "row"), "col"),
        P(("row", "col"), None),
        P(("leaf", "col"), "row"),
        P(("leaf", "col"), "row"),
        P("leaf", ("row", "col")),
        P(),
    )

    return jax.shard_map(
        shards,
        mesh=mesh,
        in_specs=placed,
        out_specs=(P(("leaf", "row"), "col"), P(("row", "col"), None)),
        check_vma=False,
    )
```

```python
import jax
import jax.numpy as jnp
from jax import lax
from jax.experimental import pallas as pl
from jax.experimental.pallas import tpu as pltpu
from jax.sharding import PartitionSpec as P


PHASES = 1
SHARES = 1, 1
KERNEL_BYTES = 24 << 20
TILE = 256
COVER = 2
F32 = jnp.float32
BF16 = jnp.bfloat16


def dot_nt(left, right):
    return lax.dot_general(left, right, (((1,), (1,)), ((), ())), preferred_element_type=F32)


def dot_nn(left, right):
    return lax.dot_general(left, right, (((1,), (0,)), ((), ())), preferred_element_type=F32)


def call(kernel, outs, index, operands, scratch, flops):
    moved = sum(a.size * a.dtype.itemsize for a in operands)
    return pl.pallas_call(
        kernel,
        out_shape=outs,
        in_specs=[pl.BlockSpec(memory_space=pltpu.SMEM)]
        + [pl.BlockSpec(memory_space=pltpu.VMEM)] * len(operands),
        out_specs=[pl.BlockSpec(memory_space=pltpu.VMEM)] * len(outs),
        scratch_shapes=scratch,
        cost_estimate=pl.CostEstimate(flops=flops, bytes_accessed=moved, transcendentals=0),
        compiler_params=pltpu.CompilerParams(vmem_limit_bytes=KERNEL_BYTES),
    )(index, *operands)


def after(value, *done):
    return lax.optimization_barrier((value, *done))[0]


def exchange(pieces, axis):
    size = lax.axis_size(axis)
    out = [pieces[0]]
    for o in range(1, size):
        out.append(lax.ppermute(pieces[o], axis, [(i, i ^ o) for i in range(size)]))
    return out


def relay(near, far, axis):
    size = lax.axis_size(axis)
    if size != 4:
        return exchange([near] + [far] * (size - 1), axis)
    out = [near, None, None, None]
    for o, piece in ((3, far), (1, near), (2, None)):
        piece = out[3] if o == 2 else piece
        out[o] = lax.ppermute(piece, axis, [(i, i ^ {1: 1, 2: 1, 3: 3}[o]) for i in range(size)])
    return out


def spread(piece, axis):
    return exchange([piece] * lax.axis_size(axis), axis)


def add_all(pieces):
    total = pieces[0].astype(F32)
    for piece in pieces[1:]:
        total = total + piece.astype(F32)
    return total


def at(index, step):
    return pl.ds(pl.multiple_of(index * step, step), step)


def shape(*dims, dtype=BF16):
    return jax.ShapeDtypeStruct(dims, dtype)


def shards(sketch_leaf, sketch_sep, leaf_inverse, coupling, sep_inverse, front_map):
    n_leaf, n_row, n_col = (lax.axis_size(a) for a in ("leaf", "row", "col"))
    assert n_row == n_col and n_row & (n_row - 1) == 0 and n_leaf & (n_leaf - 1) == 0
    n = n_row
    section, r, c = (lax.axis_index(a) for a in ("leaf", "row", "col"))
    q = r * n_col + c
    rows, width = leaf_inverse.shape
    wide = sketch_leaf.shape[1]
    blk = coupling.shape[1] * n_row // front_map.shape[1]
    span = coupling.shape[1]
    sep_rows, sep_width = sep_inverse.shape
    group = sketch_sep.shape[0] // blk
    half = rows // PHASES
    assert rows == width

    slots = [
        jnp.clip(front_map[section ^ o, q] - q * group, 0, group - 1) for o in range(n_leaf)
    ]
    index = jnp.stack([r, c] + slots).astype(jnp.int32)

    leaf_t = sketch_leaf.T
    sep_t = sketch_sep.T.reshape(n, wide, sep_width)

    def stream(h, chunk, offset):
        cols = chunk * n

        def needed(row_end, row_parts, col_parts, limit):
            last = (row_end // blk) * row_parts - 1
            return min(limit, (last // col_parts + 1) * blk)

        def first_row(col_start, row_parts, col_parts, limit):
            return min(limit, (col_start // blk) * col_parts // row_parts * blk)

        def forward_leaf(h, index):
            base = h * half
            depth = needed(base + half, n_col, n_row, width)
            assert depth <= (h + 1) * half

            def kernel(idx, inv, *refs):
                count = n * (h + 1)
                pieces, outs, lhs = refs[:count], refs[count : count + n], refs[count + n]
                for k in range(h + 1):
                    for o in range(n):
                        lhs[at(idx[0] ^ o, chunk), k * half : (k + 1) * half] = pieces[k * n + o][...]
                for start in range(0, half, TILE):
                    reach = needed(base + start + TILE, n_col, n_row, width)
                    acc = dot_nt(
                        lhs[:, :reach], inv[base + start : base + start + TILE, :reach]
                    ).astype(BF16)
                    for p in range(n):
                        outs[p][:, start : start + TILE] = acc[p * chunk : (p + 1) * chunk]

            return lambda pieces: call(
                kernel, [shape(chunk, half)] * n, index, [leaf_inverse] + pieces,
                [pltpu.VMEM((cols, (h + 1) * half), BF16)], 2 * cols * half * depth,
            )

        def forward_coupling(pieces):
            def kernel(idx, cpl, *refs):
                count = n * PHASES
                pieces, outs = refs[:count], refs[count : count + n]
                lhs, res = refs[count + n :]
                for k in range(PHASES):
                    for p in range(n):
                        place = at(idx[0] ^ idx[1] ^ p, chunk)
                        lhs[place, k * half : (k + 1) * half] = pieces[k * n + p][...]
                for s in range(0, span, TILE):
                    res[:, s : s + TILE] = dot_nn(lhs[...], cpl[:, s : s + TILE])
                for o in range(n):
                    outs[o][...] = res[:, at(idx[1] ^ o, blk)].astype(BF16)

            return call(
                kernel, [shape(cols, blk)] * n, index, [coupling] + pieces,
                [pltpu.VMEM((cols, rows), BF16), pltpu.VMEM((cols, span), F32)],
                COVER * cols * rows * span,
            )

        def sep_rhs(sketch, blocks):
            def kernel(idx, sketch, *refs):
                blocks, outs, rhs = refs[:n_leaf], refs[n_leaf:-1], refs[-1]
                rhs[...] = sketch[...].astype(F32)
                for o in range(n_leaf):
                    place = at(idx[2 + o], blk)
                    rhs[:, place] = rhs[:, place] - blocks[o][...].astype(F32)
                for k in range(n):
                    rounded = rhs[k * chunk : (k + 1) * chunk, :].astype(BF16)
                    outs[0][at(idx[0] ^ k, chunk), :] = rounded

            return call(
                kernel, [shape(cols, sep_width)], index, [sketch] + blocks,
                [pltpu.VMEM((cols, sep_width), F32)], cols * sep_width,
            )

        def forward_sep(index, base, size, rhs):
            def kernel(idx, inv, lhs, *outs):
                for start in range(0, size, TILE):
                    reach = needed(base + start + TILE, n_leaf, n_row * n_col, sep_width)
                    acc = dot_nt(
                        lhs[:, :reach], inv[base + start : base + start + TILE, :reach]
                    ).astype(BF16)
                    for p in range(n):
                        outs[p][:, start : start + TILE] = acc[p * chunk : (p + 1) * chunk]

            return call(
                kernel, [shape(chunk, size)] * n, index, [sep_inverse, rhs], [],
                2 * cols * size * sep_width,
            )

        def reduce_first(size, second, pieces):
            part = size // n

            def kernel(idx, *refs):
                pieces, outs = refs[:n], refs[n:]
                for o in range(n):
                    place = at(idx[second] ^ o, part)
                    outs[o][...] = add_all([piece[:, place] for piece in pieces]).astype(BF16)

            return call(kernel, [shape(chunk, part)] * n, index, pieces, [], n * chunk * size)

        def backward_sep(base, size, first_axis, pieces, before):
            part = size // n
            given = [] if before is None else [before]

            def kernel(idx, inv, *refs):
                pieces, before, (out, lhs) = refs[:n], refs[n:-2], refs[-2:]
                for p in range(n):
                    for o in range(n):
                        place = at(idx[first_axis] ^ p, chunk), at(idx[1 - first_axis] ^ o, part)
                        lhs[place] = pieces[p][o]
                for start in range(0, sep_width, TILE):
                    first = max(first_row(start, n_leaf, n_row * n_col, sep_rows) - base, 0)
                    stop = start + TILE
                    if first < size:
                        acc = dot_nn(lhs[:, first:], inv[base + first : base + size, start:stop])
                    else:
                        acc = jnp.zeros((cols, TILE), F32)
                    for old in before:
                        acc = acc + old[:, start:stop]
                    out[:, start:stop] = acc

            return call(
                kernel, [shape(cols, sep_width, dtype=F32)], index, [sep_inverse] + pieces + given,
                [pltpu.VMEM((cols, size), BF16)], 2 * cols * size * sep_width,
            )[0]

        def pull(parts):
            def kernel(idx, *refs):
                parts, out, pulled = refs[:n_leaf], refs[n_leaf], refs[n_leaf + 1]
                out[...] = add_all([ref[...] for ref in parts])
                pulled[...] = out[:, at(idx[2], blk)].astype(BF16)

            return call(
                kernel, [shape(cols, sep_width, dtype=F32), shape(cols, blk)], index, parts, [],
                cols * sep_width,
            )

        def backward_coupling(h, pieces):
            base = h * half

            def kernel(idx, cpl, *refs):
                pieces, outs, lhs = refs[:n], refs[n : 2 * n], refs[2 * n]
                for o in range(n):
                    for k in range(n):
                        lhs[at(idx[0] ^ idx[1] ^ k, chunk), at(idx[1] ^ o, blk)] = pieces[o][
                            k * chunk : (k + 1) * chunk, :
                        ]
                for start in range(0, half, TILE):
                    acc = dot_nt(lhs[...], cpl[base + start : base + start + TILE, :]).astype(BF16)
                    for p in range(n):
                        outs[p][:, start : start + TILE] = acc[p * chunk : (p + 1) * chunk]

            return call(
                kernel, [shape(chunk, half)] * n, index, [coupling] + pieces,
                [pltpu.VMEM((cols, span), BF16)], COVER * cols * half * span,
            )

        def backward_leaf(index, h, pieces):
            base = h * half
            later = PHASES - h

            def kernel(idx, inv, *refs):
                count = n * later
                pieces, outs, lhs = refs[:count], refs[count : count + n], refs[count + n]
                for k in range(later):
                    for p in range(n):
                        lhs[at(idx[0] ^ p, chunk), k * half : (k + 1) * half] = pieces[k * n + p][...]
                for start in range(0, half, TILE):
                    first = first_row(base + start, n_col, n_row, rows)
                    assert first >= base
                    acc = dot_nn(
                        lhs[:, first - base :], inv[first:, base + start : base + start + TILE]
                    ).astype(BF16)
                    for o in range(n):
                        outs[o][:, start : start + TILE] = acc[o * chunk : (o + 1) * chunk]

            return call(
                kernel, [shape(chunk, half)] * n, index, [leaf_inverse] + pieces,
                [pltpu.VMEM((cols, later * half), BF16)], 2 * cols * half * half * later,
            )

        source = leaf_t[offset : offset + chunk]
        if h:
            source = after(source, seen["A"][3])
        pieces = relay(source, source, "col")
        seen["A"] = pieces
        parts = forward_leaf(0, index)(pieces)
        front = add_all(exchange(parts, "row")).astype(BF16)
        parts = forward_coupling(spread(front, "row"))
        coupled = add_all(exchange(parts, "col")).astype(BF16)
        sketch = sep_t[:, offset : offset + chunk].reshape(cols, sep_width)
        rhs = sep_rhs(sketch, spread(coupled, "leaf"))
        parts = exchange(forward_sep(index, 0, sep_rows, rhs[0]), "row")
        if h:
            parts = [after(parts[0], seen["mid"])] + parts[1:]
        parts = exchange(reduce_first(sep_rows, 1, parts), "col")
        if h:
            parts = [after(parts[0], seen["stack"])] + parts[1:]
        mid = add_all(parts).astype(BF16)
        stack = jnp.stack(spread(mid, "col"))
        seen["mid"], seen["stack"] = mid, stack
        pieces = spread(stack, "row")
        total = backward_sep(0, sep_rows, 0, pieces, None)
        out_sep, pulled = pull(spread(total, "leaf"))
        parts = backward_coupling(0, spread(pulled, "col"))
        back = add_all(exchange(parts, "row"))
        leaf_rhs = (front.astype(F32) - back).astype(BF16)
        pieces = spread(leaf_rhs, "row")
        parts = backward_leaf(index, 0, pieces)
        return add_all(exchange(parts, "col")), out_sep

    seen = {}
    sizes = [wide * share // sum(SHARES) for share in SHARES]
    results = [stream(h, size, sum(sizes[:h])) for h, size in enumerate(sizes)]
    out_leaf = jnp.concatenate([leaf for leaf, _ in results], axis=0)
    out_sep = jnp.concatenate(
        [sep.reshape(n, size, sep_width) for size, (_, sep) in zip(sizes, results)], axis=1
    )
    return out_leaf.T, out_sep.reshape(sketch_sep.shape[1], sep_width).T


def solution(mesh):
    placed = (
        P(("leaf", "row"), "col"),
        P(("row", "col"), None),
        P(("leaf", "col"), "row"),
        P(("leaf", "col"), "row"),
        P("leaf", ("row", "col")),
        P(),
    )

    return jax.shard_map(
        shards,
        mesh=mesh,
        in_specs=placed,
        out_specs=(P(("leaf", "row"), "col"), P(("row", "col"), None)),
        check_vma=False,
    )
```
